32 devices in a mesh: seq: 4 (over z), fsdp: 8 (over y, x, core).
Axes of the slice: x: 2, y: 2, z: 4, core: 2. Of those that a mesh axis runs over, the one named last changes fastest.
Arguments:
- tokens: bfloat16 [2048, 4096], P('seq', 'fsdp'), may hold values from -6 to 6
- in_mask: int32 [2048, 4096], P('seq', 'fsdp'), may hold values 0 or 1
- out_mask: int32 [2048, 8, 384], P('seq', 'fsdp'), may hold values 0 or 1
- w_mean: bfloat16 [4096, 8, 384], P('seq', 'fsdp'), may hold values from -0.09375 to 0.09375
- w_sigma: bfloat16 [4096, 8, 384], P('seq', 'fsdp'), may hold values from -0.046875 to 0.046875
- grad_out: bfloat16 [2048, 1024], P('seq', 'fsdp'), may hold values from -6 to 6
Outputs:
- attended: bfloat16 [2048, 1024], P('seq', 'fsdp')
- d_tokens: bfloat16 [2048, 4096], P('seq', 'fsdp')
- g_mean: bfloat16 [4096, 8, 384], P('seq', 'fsdp')
- g_sigma: bfloat16 [4096, 8, 384], P('seq', 'fsdp')
The draws below stay inside these ranges and needn't reach their ends.
Inputs may be any that keep to these rules, and one draw needn't show every extreme that they name: `in_mask`: each entry is a sign bit: the sign is 2 * entry - 1. `out_mask`: each entry is a sign bit: the sign is 2 * entry - 1.
All inputs are finite; a program needn't handle non-finite values. No bound on the sum of `in_mask` or of `out_mask` on one device may be relied on, other than what follows from the above.
Results may differ from the reference program's by a relative error of at most 0.017.
Values may be sent and summed in bfloat16 or wider, within the bound.
No kernel may reach another device: no remote copies, remote signals or barrier semaphores. Data moves between devices by JAX's collectives and lax.ppermute only.
A program may use at most 64 MiB of HBM per device.

```python
import jax
import jax.numpy as jnp
from jax import lax

D = 4096
E = 128
HEADS_DEV = 1
TOK_DEV = 512
H = 8
S = 2048
N_SEQ = 4
N_FSDP = 8


def place_ends(drawn, key, least, largest):
    dims = drawn.shape
    spot = [jax.random.randint(jax.random.fold_in(key, axis), (), 0, dims[axis]) for axis in range(len(dims))]
    drawn = drawn.at[tuple(spot)].set(least)
    longest = dims.index(max(dims))
    spot[longest] = (spot[longest] + 1) % dims[longest]
    return drawn.at[tuple(spot)].set(largest)


def shard_levels(stream_key, dims, pieces, least, high):
    def one(dim, shards_of):
        draws = jax.random.uniform(jax.random.fold_in(jax.random.fold_in(stream_key, 6), dim), (shards_of,), jnp.float32, least / len(pieces), high / len(pieces))
        return jnp.repeat(jnp.exp(draws), dims[dim] // shards_of).reshape((-1,) + (1,) * (len(dims) - dim - 1))

    level = one(*pieces[0])
    for cut in pieces[1:]:
        level = level * one(*cut)
    return level


def gaussian(key, shape, deviation, most, shards=(), dtype=jnp.bfloat16):
    array = deviation * jax.random.normal(key, shape, jnp.float32)
    if shards:
        array = array * shard_levels(key, shape, shards, -0.22, 0.18)
    return jnp.clip(array, -most, most).astype(dtype)


def setup_inputs(seed: int = 0) -> dict:
    keys = jax.random.split(jax.random.key(seed), 7)
    tokens = gaussian(keys[0], (S, D), 1.0, 6.0, ((0, 4), (1, 8)))
    in_mask = place_ends((jax.random.randint(keys[1], (S, D), 0, 2) < 1).astype(jnp.int32), jax.random.fold_in(keys[1], 1), 0, 1)
    out_mask = place_ends((jax.random.randint(keys[2], (S, H, 3 * E), 0, 2) < 1).astype(jnp.int32), jax.random.fold_in(keys[2], 1), 0, 1)
    w_mean = gaussian(keys[3], (D, H, 3 * E), D ** -0.5, 0.09375, ((0, 4), (1, 8)))
    w_sigma = gaussian(keys[4], (D, H, 3 * E), (4 * D) ** -0.5, 0.046875, ((0, 4), (1, 8)))
    grad_out = gaussian(keys[5], (S, H * E), 1.0, 6.0, ((0, 4), (1, 8)))
    return {"tokens": tokens, "in_mask": in_mask, "out_mask": out_mask, "w_mean": w_mean, "w_sigma": w_sigma, "grad_out": grad_out}


EPSILON = 1e-06

def feature_map(u):
    return jnp.where(u > 0, u + 1.0, jnp.exp(jnp.minimum(u, 0.0)))

def feature_slope(u):
    return jnp.where(u > 0, 1.0, jnp.exp(jnp.minimum(u, 0.0)))

def head_pass(pair):
    highest = lax.Precision.HIGHEST
    projected_head, upstream_head = pair
    seq_len = projected_head.shape[0]
    blocks = seq_len // TOK_DEV
    pre_query = projected_head[:, :E]
    pre_keys = projected_head[:, E:2 * E]
    queries = feature_map(pre_query)
    key_feats = feature_map(pre_keys)
    values = projected_head[:, 2 * E:]
    causal = (lax.broadcasted_iota(jnp.int32, (TOK_DEV, TOK_DEV), 0) >= lax.broadcasted_iota(jnp.int32, (TOK_DEV, TOK_DEV), 1)).astype(jnp.float32)
    q_blocks = queries.reshape(blocks, TOK_DEV, E)
    k_blocks = key_feats.reshape(blocks, TOK_DEV, E)
    v_blocks = values.reshape(blocks, TOK_DEV, E)

    def forward_step(state, block):
        q_blk, k_blk, v_blk = block
        scores = jnp.dot(q_blk, k_blk.T, precision=highest) * causal
        numer = jnp.dot(scores, v_blk, precision=highest) + jnp.dot(q_blk, state, precision=highest)
        return (state + jnp.dot(k_blk.T, v_blk, precision=highest), (numer, state))
    start_state = jnp.zeros((E, E), jnp.float32)
    last_state, (numerator, incoming) = lax.scan(forward_step, start_state, (q_blocks, k_blocks, v_blocks))
    numerator = numerator.reshape(seq_len, E)
    inv_norm = lax.rsqrt(lax.optimization_barrier(jnp.mean(numerator * numerator, axis=-1, keepdims=True)) + EPSILON)
    normed = numerator * inv_norm
    d_numer = inv_norm * (upstream_head - normed * lax.optimization_barrier(jnp.mean(upstream_head * normed, axis=-1, keepdims=True)))
    dn_blocks = d_numer.reshape(blocks, TOK_DEV, E)

    def backward_step(suffix, block):
        q_blk, k_blk, v_blk, dn_blk, state_in = block
        scores = jnp.dot(q_blk, k_blk.T, precision=highest) * causal
        d_scores = jnp.dot(dn_blk, v_blk.T, precision=highest) * causal
        d_query = jnp.dot(d_scores, k_blk, precision=highest) + jnp.dot(dn_blk, state_in.T, precision=highest)
        d_keys = jnp.dot(d_scores.T, q_blk, precision=highest) + jnp.dot(v_blk, suffix.T, precision=highest)
        d_values = jnp.dot(scores.T, dn_blk, precision=highest) + jnp.dot(k_blk, suffix, precision=highest)
        return (suffix + jnp.dot(q_blk.T, dn_blk, precision=highest), (d_query, d_keys, d_values))
    last_suffix, (d_query, d_keys, d_values) = lax.scan(backward_step, start_state, (q_blocks, k_blocks, v_blocks, dn_blocks, incoming), reverse=True)
    d_query = d_query.reshape(seq_len, E) * feature_slope(pre_query)
    d_keys = d_keys.reshape(seq_len, E) * feature_slope(pre_keys)
    d_values = d_values.reshape(seq_len, E)
    return (normed, jnp.concatenate([d_query, d_keys, d_values], axis=-1))

def reference(tokens, in_mask, out_mask, w_mean, w_sigma, grad_out):
    seq_len = tokens.shape[0]
    columns = H * 3 * E
    in_sign = (2 * in_mask - 1).astype(jnp.bfloat16)
    flipped = tokens * in_sign
    out_sign = (2 * out_mask - 1).astype(jnp.float32)
    projected = jnp.dot(tokens, w_mean.reshape(D, columns), preferred_element_type=jnp.float32)
    projected = projected + jnp.dot(flipped, w_sigma.reshape(D, columns), preferred_element_type=jnp.float32) * out_sign.reshape(seq_len, columns)
    projected = jnp.transpose(projected.reshape(seq_len, H, 3 * E), (1, 0, 2))
    upstream = jnp.transpose(grad_out.astype(jnp.float32).reshape(seq_len, H, E), (1, 0, 2))
    normed, grad_pre = lax.map(head_pass, (projected, upstream))
    attended = jnp.transpose(normed, (1, 0, 2)).reshape(seq_len, H * E).astype(jnp.bfloat16)
    grad_mean = jnp.transpose(grad_pre, (1, 0, 2)).astype(jnp.bfloat16)
    grad_sigma = grad_mean * out_sign.astype(jnp.bfloat16)
    gm_flat = grad_mean.reshape(seq_len, columns)
    gs_flat = grad_sigma.reshape(seq_len, columns)

    def weight_step(running, block):
        tok_block, flip_block, gm_block, gs_block = block
        part_mean = jnp.dot(tok_block.T, gm_block, preferred_element_type=jnp.float32)
        part_sigma = jnp.dot(flip_block.T, gs_block, preferred_element_type=jnp.float32)
        part_mean = lax.optimization_barrier(part_mean.astype(jnp.bfloat16)).astype(jnp.float32)
        part_sigma = lax.optimization_barrier(part_sigma.astype(jnp.bfloat16)).astype(jnp.float32)
        return ((running[0] + part_mean, running[1] + part_sigma), None)
    zero_weights = jnp.zeros((D, columns), jnp.float32)
    (sum_mean, sum_sigma), unused = lax.scan(weight_step, (zero_weights, zero_weights), (tokens.reshape(N_SEQ, TOK_DEV, D), flipped.reshape(N_SEQ, TOK_DEV, D), gm_flat.reshape(N_SEQ, TOK_DEV, columns), gs_flat.reshape(N_SEQ, TOK_DEV, columns)))
    group_cols = HEADS_DEV * 3 * E
    gm_groups = jnp.transpose(gm_flat.reshape(seq_len, N_FSDP, group_cols), (1, 0, 2))
    gs_groups = jnp.transpose(gs_flat.reshape(seq_len, N_FSDP, group_cols), (1, 0, 2))
    wm_groups = jnp.transpose(w_mean.reshape(D, N_FSDP, group_cols), (1, 0, 2))
    ws_groups = jnp.transpose(w_sigma.reshape(D, N_FSDP, group_cols), (1, 0, 2))

    def input_step(running, group):
        gm_group, gs_group, wm_group, ws_group = group
        term_mean = jnp.dot(gm_group, wm_group.T, preferred_element_type=jnp.float32)
        term_sigma = jnp.dot(gs_group, ws_group.T, preferred_element_type=jnp.float32)
        term_mean = lax.optimization_barrier(term_mean.astype(jnp.bfloat16)).astype(jnp.float32)
        term_sigma = lax.optimization_barrier(term_sigma.astype(jnp.bfloat16)).astype(jnp.float32)
        return ((running[0] + term_mean, running[1] + term_sigma), None)
    zero_inputs = jnp.zeros((seq_len, D), jnp.float32)
    (back_mean, back_sigma), unused_two = lax.scan(input_step, (zero_inputs, zero_inputs), (gm_groups, gs_groups, wm_groups, ws_groups))
    d_tokens = (back_mean + in_sign.astype(jnp.float32) * back_sigma).astype(jnp.bfloat16)
    g_mean = sum_mean.reshape(D, H, 3 * E).astype(jnp.bfloat16)
    g_sigma = sum_sigma.reshape(D, H, 3 * E).astype(jnp.bfloat16)
    return (attended, d_tokens, g_mean, g_sigma)
```

```python
import jax
import jax.numpy as jnp
from jax import lax
from jax.sharding import PartitionSpec as P

EPSILON = 1e-06
AXES = ("seq", "fsdp")


def feature_map(u):
    return jnp.where(u > 0, u + 1.0, jnp.exp(jnp.minimum(u, 0.0)))


def feature_slope(u):
    return jnp.where(u > 0, 1.0, jnp.exp(jnp.minimum(u, 0.0)))


def xor_order(x, index, axis):
    size = x.shape[axis]
    bit = 1
    while bit < size:
        shape = x.shape[:axis] + (size // (2 * bit), 2, bit) + x.shape[axis + 1 :]
        flipped = jnp.flip(x.reshape(shape), axis + 1).reshape(x.shape)
        x = jnp.where((index & bit) != 0, flipped, x)
        bit *= 2
    return x


def dot(a, b, dims):
    return lax.dot_general(a, b, (dims, ((), ())), preferred_element_type=jnp.float32)


def make_local(n_seq, n_fsdp):
    half = n_seq // 2
    n_mid = n_fsdp // 4
    per_block = n_mid // half

    def send(x, target):
        pairs = []
        for z in range(n_seq):
            for f in range(n_fsdp):
                to = target(z, f)
                if to is not None:
                    pairs.append((z * n_fsdp + f, to[0] * n_fsdp + to[1]))
        return lax.ppermute(x, AXES, pairs)

    top = n_fsdp // 2

    def moves(z, f):
        return (f // top) != (z // half)

    def core(x):
        return send(x, lambda z, f: (z, f ^ 1))

    def plane(x, mask):
        return send(x, lambda z, f: (z, f ^ mask))

    def far(x):
        return send(x, lambda z, f: (z ^ half, f))

    def near(x, mask):
        return send(x, lambda z, f: (z ^ mask, f))

    def local(tokens, in_mask, out_mask, w_mean, w_sigma, grad_out):
        highest = lax.Precision.HIGHEST
        bf16, f32 = jnp.bfloat16, jnp.float32
        rows, width = tokens.shape
        head_count = w_mean.shape[1]
        columns = head_count * w_mean.shape[2]
        head_width = w_mean.shape[2] // 3
        z = lax.axis_index("seq")
        f = lax.axis_index("fsdp")
        z_high, z_low = z // half, z % half
        is_core, mid = f % 2, (f // 2) % n_mid
        stays = (f // top) == z_high

        in_sign = (2 * in_mask - 1).astype(bf16)
        tokens_moved = send(tokens, lambda z, f: (z ^ half, f ^ top) if moves(z, f) else None)
        sign_side = send(in_sign, lambda z, f: (z, f ^ top) if moves(z, f) else None)
        sign_moved = send(sign_side, lambda z, f: None if moves(z, f) else (z ^ half, f))

        pair = jnp.stack([w_mean.reshape(-1, columns), w_sigma.reshape(-1, columns)])
        pair = pair.reshape(2, per_block, 2, width, columns)
        mine = lax.dynamic_index_in_dim(pair, is_core, 2, keepdims=False)
        theirs = lax.dynamic_index_in_dim(pair, 1 - is_core, 2, keepdims=False)
        wide = jnp.concatenate([mine, core(theirs)], axis=-1)
        blocks = [wide] + [near(wide, m) for m in range(1, half)]
        panel = jnp.stack(blocks, axis=1)
        panel = xor_order(panel, (mid // per_block) ^ z_low, 1)
        panel = xor_order(panel, mid % per_block, 2)
        panel = panel.reshape(2, n_mid, width, 2 * columns)

        def gather(x):
            near_side = [x] + [plane(x, 2 * j) for j in range(1, n_mid)]
            across = plane(x, top)
            cut = rows // 2
            far_side = [across]
            for j in range(1, n_mid):
                upper = plane(near_side[j][:cut], top)
                lower = plane(across[cut:], 2 * j)
                far_side.append(jnp.concatenate([upper, lower], axis=0))
            return [near_side, far_side]

        own_tokens = jnp.where(stays, tokens, tokens_moved)
        token_parts = gather(own_tokens)
        own_sign = jnp.where(stays, in_sign, sign_moved)
        sign_parts = gather(own_sign)

        out_own = (2 * out_mask - 1).astype(bf16).reshape(rows, columns)
        out_far = far(out_own)
        out_both = jnp.stack([jnp.where(stays, out_own, out_far), jnp.where(stays, out_far, out_own)])
        out_sign = jnp.concatenate([out_both, core(out_both)], axis=-1)

        flip_parts = [[t * s for t, s in zip(ts, ss)] for ts, ss in zip(token_parts, sign_parts)]
        partial = []
        for i in range(2):
            mean = sum(dot(token_parts[i][j], panel[0, j], ((1,), (0,))) for j in range(n_mid))
            sigma = sum(dot(flip_parts[i][j], panel[1, j], ((1,), (0,))) for j in range(n_mid))
            partial.append(mean + out_sign[i].astype(f32) * sigma)
        part_own = jnp.where(stays, partial[0], partial[1])
        part_far = jnp.where(stays, partial[1], partial[0])
        chip_far = part_far[:, :columns] + core(part_far[:, columns:].astype(bf16)).astype(f32)
        from_far = far(chip_far.astype(bf16))
        chip_own = part_own[:, :columns] + core(part_own[:, columns:].astype(bf16)).astype(f32)
        projected = chip_own + from_far.astype(f32)
        projected = projected.reshape(rows, head_count, 3 * head_width).transpose(1, 0, 2)

        pre_query = projected[:, :, :head_width]
        pre_keys = projected[:, :, head_width : 2 * head_width]
        queries = feature_map(pre_query)
        key_feats = feature_map(pre_keys)
        values = projected[:, :, 2 * head_width :]
        causal = (
            lax.broadcasted_iota(jnp.int32, (rows, rows), 0)
            >= lax.broadcasted_iota(jnp.int32, (rows, rows), 1)
        ).astype(f32)
        state = jnp.einsum("hse,hsf->hef", key_feats, values, precision=highest).astype(bf16)
        incoming = sum(
            send(state, lambda z, f, k=k: (z + k, f) if z + k < n_seq else None).astype(f32)
            for k in range(1, n_seq)
        )
        scores = jnp.einsum("hte,hse->hts", queries, key_feats, precision=highest) * causal
        numerator = jnp.einsum("hts,hsf->htf", scores, values, precision=highest)
        numerator = numerator + jnp.einsum("hte,hef->htf", queries, incoming, precision=highest)
        inv_norm = lax.rsqrt(jnp.mean(numerator * numerator, axis=-1, keepdims=True) + EPSILON)
        normed = numerator * inv_norm
        attended = normed.transpose(1, 0, 2).reshape(rows, head_count * head_width).astype(bf16)
        upstream = grad_out.astype(f32).reshape(rows, head_count, head_width).transpose(1, 0, 2)
        d_numer = inv_norm * (upstream - normed * jnp.mean(upstream * normed, axis=-1, keepdims=True))
        back_state = jnp.einsum("hte,htf->hef", queries, d_numer, precision=highest).astype(bf16)
        suffix = sum(
            send(back_state, lambda z, f, k=k: (z - k, f) if z >= k else None).astype(f32)
            for k in range(1, n_seq)
        )
        d_scores = jnp.einsum("htf,hsf->hts", d_numer, values, precision=highest) * causal
        d_query = jnp.einsum("hts,hse->hte", d_scores, key_feats, precision=highest)
        d_query = d_query + jnp.einsum("hef,htf->hte", incoming, d_numer, precision=highest)
        d_keys = jnp.einsum("hts,hte->hse", d_scores, queries, precision=highest)
        d_keys = d_keys + jnp.einsum("hef,hsf->hse", suffix, values, precision=highest)
        d_values = jnp.einsum("hts,htf->hsf", scores, d_numer, precision=highest)
        d_values = d_values + jnp.einsum("hef,hse->hsf", suffix, key_feats, precision=highest)
        grad_pre = jnp.concatenate(
            [d_query * feature_slope(pre_query), d_keys * feature_slope(pre_keys), d_values], axis=-1
        )
        grad_own = grad_pre.transpose(1, 0, 2).reshape(rows, columns).astype(bf16)

        own_wide = jnp.concatenate([grad_own, core(grad_own)], axis=-1)
        grad_far = far(grad_own)
        far_wide = jnp.concatenate([grad_far, core(grad_far)], axis=-1)
        grad_mean = [jnp.where(stays, own_wide, far_wide), jnp.where(stays, far_wide, own_wide)]
        grad_sigma = [grad_mean[i] * out_sign[i] for i in range(2)]

        grads = jnp.stack(
            [
                jnp.stack([sum(dot(parts[i][j], g[i], ((0,), (0,))) for i in range(2)) for j in range(n_mid)])
                for parts, g in ((token_parts, grad_mean), (flip_parts, grad_sigma))
            ]
        )
        grads = grads.reshape(2, half, per_block, width, 2 * columns)
        grads = xor_order(grads, mid % per_block, 2)
        grads = xor_order(grads, (mid // per_block) ^ z_low, 1)
        total = grads[:, 0]
        for m in range(1, half):
            total = total + near(grads[:, m].astype(bf16), m).astype(f32)
        total = total.astype(bf16)
        kept, given = total[..., :columns], core(total[..., columns:])
        both = jnp.stack([jnp.where(is_core == 0, kept, given), jnp.where(is_core == 0, given, kept)], axis=2)
        g_mean, g_sigma = (both[k].reshape(w_mean.shape) for k in range(2))

        sums = None
        for i in range(2):
            for j in range(n_mid):
                back = dot(grad_mean[i], panel[0, j], ((1,), (1,)))
                back = back + sign_parts[i][j].astype(f32) * dot(grad_sigma[i], panel[1, j], ((1,), (1,)))
                mask = i * top + 2 * j
                if mask:
                    back = plane(back.astype(bf16), mask).astype(f32)
                sums = back if sums is None else sums + back
        own_back = sums.astype(bf16)
        returned = send(own_back, lambda z, f: (z ^ half, f ^ top) if moves(z, f) else None)
        d_tokens = jnp.where(stays, own_back, returned)
        return attended, d_tokens, g_mean, g_sigma

    return local


def solution(mesh):
    placed = (
        P("seq", "fsdp"),
        P("seq", "fsdp"),
        P("seq", "fsdp", None),
        P("seq", "fsdp", None),
        P("seq", "fsdp", None),
        P("seq", "fsdp"),
    )
    return jax.shard_map(
        make_local(mesh.shape["seq"], mesh.shape["fsdp"]),
        mesh=mesh,
        in_specs=placed,
        out_specs=(
            P("seq", "fsdp"),
            P("seq", "fsdp"),
            P("seq", "fsdp", None),
            P("seq", "fsdp", None),
        ),
        check_vma=False,
    )
```

```python
import jax
import jax.numpy as jnp
from jax import lax
from jax.sharding import PartitionSpec as P


EPSILON = 1e-06
AXES = ("seq", "fsdp")
CHUNKS = 2
SIGN_CHUNKS = 2


def feature_map(u):
    return jnp.where(u > 0, u + 1.0, jnp.exp(jnp.minimum(u, 0.0)))


def feature_slope(u):
    return jnp.where(u > 0, 1.0, jnp.exp(jnp.minimum(u, 0.0)))


def xor_list(xs, index):
    bit = 1
    while bit < len(xs):
        swap = (index & bit) != 0
        xs = [jnp.where(swap, xs[i ^ bit], xs[i]) for i in range(len(xs))]
        bit *= 2
    return xs


def pick(flag, a, b):
    flag, a, b = lax.optimization_barrier((flag, a, b))
    return jnp.where(flag, a, b)


def dot(a, b, dims):
    return lax.dot_general(a, b, (dims, ((), ())), preferred_element_type=jnp.float32)


def make_local(n_seq, n_fsdp):
    half = n_seq // 2
    n_mid = n_fsdp // 4
    per_block = n_mid // half

    def send(x, target):
        pairs = []
        for z in range(n_seq):
            for f in range(n_fsdp):
                to = target(z, f)
                if to is not None:
                    pairs.append((z * n_fsdp + f, to[0] * n_fsdp + to[1]))
        return lax.ppermute(x, AXES, pairs)

    top = n_fsdp // 2

    def moves(z, f):
        return (f // top) != (z // half)

    def core(x):
        return send(x, lambda z, f: (z, f ^ 1))

    def plane(x, mask):
        return send(x, lambda z, f: (z, f ^ mask))

    def far(x):
        return send(x, lambda z, f: (z ^ half, f))

    def near(x, mask):
        return send(x, lambda z, f: (z ^ mask, f))

    def local(tokens, in_mask, out_mask, w_mean, w_sigma, grad_out):
        highest = lax.Precision.HIGH
        bf16, f32 = jnp.bfloat16, jnp.float32
        rows, width = tokens.shape
        head_count = w_mean.shape[1]
        columns = head_count * w_mean.shape[2]
        head_width = w_mean.shape[2] // 3
        z = lax.axis_index("seq")
        f = lax.axis_index("fsdp")
        z_high, z_low = z // half, z % half
        is_core, mid = f % 2, (f // 2) % n_mid
        stays = (f // top) == z_high

        near_mean = [near(w_mean, m) for m in range(1, half)]

        in_sign = (2 * in_mask - 1).astype(bf16)
        token_far = send(tokens, lambda z, f: (z ^ half, f ^ top) if moves(z, f) else None)
        chunk = rows // SIGN_CHUNKS
        sign_chunks = lax.optimization_barrier([in_sign[c * chunk : (c + 1) * chunk] for c in range(SIGN_CHUNKS)])
        sides = [send(x, lambda z, f: (z, f ^ top) if moves(z, f) else None) for x in sign_chunks]
        sign_far = [send(x, lambda z, f: None if moves(z, f) else (z ^ half, f)) for x in sides]

        near_sigma = [near(w_sigma, m) for m in range(1, half)]
        out_own = lax.optimization_barrier((2 * out_mask - 1).astype(bf16).reshape(rows, columns))
        out_arrived = far(out_own)
        out_near = [near(out_own, m) for m in range(1, half)]

        def gather(x):
            cut = x.shape[0] // 2
            across = plane(x, top)
            along = [plane(x, 2 * j) for j in range(1, n_mid)]
            pieces = [(x, across)]
            for j, piece in enumerate(along, 1):
                upper = plane(piece[:cut], top)
                lower = plane(across[cut:], 2 * j)
                pieces.append((piece, jnp.concatenate([upper, lower], axis=0)))
            own, other = [], []
            for a, b in pieces:
                flag, a, b = lax.optimization_barrier((stays, a, b))
                own.append(jnp.where(flag, a, b))
                other.append(jnp.where(flag, b, a))
            return own, other

        token_piece = pick(stays, tokens, token_far)
        tokens_own, tokens_far = gather(token_piece)
        signs = []
        for c in range(SIGN_CHUNKS):
            piece = pick(stays, sign_chunks[c], sign_far[c])
            signs.append(gather(piece))
        signs_own, signs_far = (
            [jnp.concatenate([signs[c][k][j] for c in range(SIGN_CHUNKS)]) for j in range(n_mid)] for k in range(2)
        )
        own_parts, far_parts = list(zip(tokens_own, signs_own)), list(zip(tokens_far, signs_far))
        cut = rows // 2

        order = mid ^ (z_low * per_block)

        def panel_of(blocks):
            pair = jnp.stack(blocks).reshape(n_mid, 2, width, columns)
            mine = lax.dynamic_index_in_dim(pair, is_core, 1, keepdims=False)
            theirs = lax.dynamic_index_in_dim(pair, 1 - is_core, 1, keepdims=False)
            theirs = core(theirs)
            return xor_list([jnp.concatenate([mine[i], theirs[i]], axis=-1) for i in range(n_mid)], order)

        panel = list(zip(panel_of([w_mean, *near_mean]), panel_of([w_sigma, *near_sigma])))

        high = f // top
        share = rows // n_mid
        ordered = [(xor_list(own, order), xor_list(other, order)) for own, other in ((tokens_own, tokens_far), (signs_own, signs_far))]

        def bring(m, own, other):
            parts = []
            for q in range(per_block):
                i = m * per_block + q
                whole = pick(high == 0, own[i], other[i])
                parts.append(lax.dynamic_slice_in_dim(whole, mid * share, share))
            parts = jnp.stack(parts)
            return near(parts, m)

        brought = [(bring(m, *ordered[0]), bring(m, *ordered[1])) for m in range(1, half)]

        out_pair = jnp.stack([out_own, out_arrived])
        out_near = [(x, near(out_arrived, m)) for m, x in enumerate(out_near, 1)]
        out_near = [jnp.stack(lax.optimization_barrier(x)) for x in out_near]
        near_sign = [jnp.concatenate([x, core(x)], axis=-1) for x in out_near]
        out_sign = jnp.concatenate([out_pair, core(out_pair)], axis=-1)

        chunk = rows // CHUNKS

        def project(parts, k, c):
            part = slice(c * chunk, (c + 1) * chunk)
            mean = sum(dot(x[0][part], w[0], ((1,), (0,))) for x, w in zip(parts, panel))
            flipped = [x[0][part] * x[1][part] for x in parts]
            sigma = sum(dot(x, w[1], ((1,), (0,))) for x, w in zip(flipped, panel))
            both = mean + out_sign[k][part].astype(f32) * sigma
            return both[:, :columns] + core(both[:, columns:].astype(bf16)).astype(f32)

        from_far = []
        for c in range(CHUNKS):
            part = project(far_parts, 1, c)
            from_far.append(far(part.astype(bf16)))
        projected = jnp.concatenate([project(own_parts, 0, c) + from_far[c].astype(f32) for c in range(CHUNKS)])
        projected = projected.reshape(rows, head_count, 3 * head_width).transpose(1, 0, 2)

        near_pieces = []
        for x in brought:
            x = jnp.stack(lax.optimization_barrier(x))
            across = plane(x, top)
            along = [plane(x, 2 * j) for j in range(1, n_mid)]
            ends = [y[:, :, : share // 2] for y in along]
            start = across[:, :, share // 2 :]
            upper = [plane(y, top) for y in ends]
            lower = [plane(start, 2 * j) for j in range(1, n_mid)]
            near_pieces.append((x, across, along, upper, lower))

        pre_query = projected[:, :, :head_width]
        pre_keys = projected[:, :, head_width : 2 * head_width]
        queries = feature_map(pre_query)
        key_feats = feature_map(pre_keys)
        values = projected[:, :, 2 * head_width :]
        causal = (
            lax.broadcasted_iota(jnp.int32, (rows, rows), 0)
            >= lax.broadcasted_iota(jnp.int32, (rows, rows), 1)
        ).astype(f32)
        state = jnp.einsum("hse,hsf->hef", key_feats, values, precision=highest).astype(bf16)
        incoming = sum(
            jnp.where(z >= k, send(state, lambda z, f, k=k: ((z + k) % n_seq, f)).astype(f32), 0.0)
            for k in range(1, n_seq)
        )
        scores = jnp.einsum("hte,hse->hts", queries, key_feats, precision=highest) * causal
        numerator = jnp.einsum("hts,hsf->htf", scores, values, precision=highest)
        numerator = numerator + jnp.einsum("hte,hef->htf", queries, incoming, precision=highest)
        inv_norm = lax.rsqrt(jnp.mean(numerator * numerator, axis=-1, keepdims=True) + EPSILON)
        normed = numerator * inv_norm
        attended = normed.transpose(1, 0, 2).reshape(rows, head_count * head_width).astype(bf16)
        upstream = grad_out.astype(f32).reshape(rows, head_count, head_width).transpose(1, 0, 2)
        d_numer = inv_norm * (upstream - normed * jnp.mean(upstream * normed, axis=-1, keepdims=True))
        back_state = jnp.einsum("hte,htf->hef", queries, d_numer, precision=highest).astype(bf16)
        suffix = sum(
            jnp.where(z + k < n_seq, send(back_state, lambda z, f, k=k: ((z - k) % n_seq, f)).astype(f32), 0.0)
            for k in range(1, n_seq)
        )
        d_scores = jnp.einsum("htf,hsf->hts", d_numer, values, precision=highest) * causal
        d_query = jnp.einsum("hts,hse->hte", d_scores, key_feats, precision=highest)
        d_query = d_query + jnp.einsum("hef,htf->hte", incoming, d_numer, precision=highest)
        d_keys = jnp.einsum("hts,hte->hse", d_scores, queries, precision=highest)
        d_keys = d_keys + jnp.einsum("hef,hsf->hse", suffix, values, precision=highest)
        d_values = jnp.einsum("hts,htf->hsf", scores, d_numer, precision=highest)
        d_values = d_values + jnp.einsum("hef,hse->hsf", suffix, key_feats, precision=highest)
        grad_pre = jnp.concatenate(
            [d_query * feature_slope(pre_query), d_keys * feature_slope(pre_keys), d_values], axis=-1
        )
        grad_own = grad_pre.transpose(1, 0, 2).reshape(rows, columns).astype(bf16)

        near_own = [near(grad_own, m) for m in range(1, half)]
        grad_far = far(grad_own)
        near_far = [near(grad_far, m) for m in range(1, half)]

        def widened(grad, sign):
            wide, sign = lax.optimization_barrier((jnp.concatenate([grad, core(grad)], axis=-1), sign))
            return wide, wide * sign

        own_wide, far_wide = widened(grad_own, out_sign[0]), widened(grad_far, out_sign[1])
        wides, flips = zip(own_wide, far_wide)

        def row_sum(parts, k):
            sums = None
            for j in range(n_mid):
                back = dot(wides[k], panel[j][0], ((1,), (1,)))
                back = back + parts[j][1].astype(f32) * dot(flips[k], panel[j][1], ((1,), (1,)))
                if j:
                    back = plane(back.astype(bf16), 2 * j).astype(f32)
                sums = back if sums is None else sums + back
            return sums

        own_sum = row_sum(own_parts, 0)
        own_y = send(own_sum.astype(bf16), lambda z, f: (z, f ^ top) if moves(z, f) else None)
        own_sum = own_sum + own_y.astype(f32)

        far_half = None
        for j in reversed(range(n_mid)):
            back = dot(far_wide[0], panel[j][0], ((1,), (1,)))
            back = back + far_parts[j][1].astype(f32) * dot(far_wide[1], panel[j][1], ((1,), (1,)))
            mine = jnp.where(stays, back[:cut], back[cut:])
            other = jnp.where(stays, back[cut:], back[:cut]).astype(bf16)
            arrived = plane(other, top + 2 * j).astype(f32)
            if j:
                arrived = arrived + plane(mine.astype(bf16), 2 * j).astype(f32)
            else:
                arrived = arrived + mine
            far_half = arrived if far_half is None else far_half + arrived
        far_half = far_half.astype(bf16)
        last_back = other
        first = send(far_half, lambda z, f: None if moves(z, f) else (z ^ half, f))
        second = send(far_half, lambda z, f: (z ^ half, f ^ top) if moves(z, f) else None)
        d_tokens = jnp.where(stays, own_sum.astype(bf16), jnp.concatenate([first, second], axis=0))
        near_rows = []
        for pieces in near_pieces:
            x, across, along, upper, lower = lax.optimization_barrier((pieces, last_back))[0]
            mine = jnp.concatenate(xor_list([x, *along], mid), axis=2)
            ends = [jnp.concatenate(pair, axis=2) for pair in zip(upper, lower)]
            other = jnp.concatenate(xor_list([across, *ends], mid), axis=2)
            near_rows.append((jnp.where(high == 0, mine, other), jnp.where(high == 0, other, mine)))
        terms = [(own_wide, [(ordered[0][0][q], ordered[1][0][q]) for q in range(per_block)])]
        terms.append((far_wide, [(ordered[0][1][q], ordered[1][1][q]) for q in range(per_block)]))
        for grads, k in ((near_own, 0), (near_far, 1)):
            for grad, sign, pieces in zip(grads, near_sign, near_rows):
                pair = [(pieces[k][0, q], pieces[k][1, q]) for q in range(per_block)]
                terms.append((widened(grad, sign[k]), pair))
        sums = None
        for g, x in terms:
            part = [dot(x[q][0], g[0], ((0,), (0,))) for q in range(per_block)]
            part += [dot(x[q][0] * x[q][1], g[1], ((0,), (0,))) for q in range(per_block)]
            sums = part if sums is None else [a + b for a, b in zip(sums, part)]
        total = jnp.stack(sums).reshape(2, per_block, width, 2 * columns).astype(bf16)
        kept, given = total[..., :columns], core(total[..., columns:])
        full = jnp.stack([jnp.where(is_core == 0, kept, given), jnp.where(is_core == 0, given, kept)], axis=2)
        g_mean, g_sigma = (full[k].reshape(w_mean.shape) for k in range(2))
        return attended, d_tokens, g_mean, g_sigma

    return local


def solution(mesh):
    placed = (
        P("seq", "fsdp"),
        P("seq", "fsdp"),
        P("seq", "fsdp", None),
        P("seq", "fsdp", None),
        P("seq", "fsdp", None),
        P("seq", "fsdp"),
    )
    return jax.shard_map(
        make_local(mesh.shape["seq"], mesh.shape["fsdp"]),
        mesh=mesh,
        in_specs=placed,
        out_specs=(
            P("seq", "fsdp"),
            P("seq", "fsdp"),
            P("seq", "fsdp", None),
            P("seq", "fsdp", None),
        ),
        check_vma=False,
    )
```

```python
import jax
import jax.numpy as jnp
from jax import lax
from jax.sharding import PartitionSpec as P


EPSILON = 1e-06
AXES = ("seq", "fsdp")
CHUNKS = 2
SIGN_CHUNKS = 2


def feature_map(u):
    return jnp.where(u > 0, u + 1.0, jnp.exp(jnp.minimum(u, 0.0)))


def feature_slope(u):
    return jnp.where(u > 0, 1.0, jnp.exp(jnp.minimum(u, 0.0)))


def xor_list(xs, index):
    bit = 1
    while bit < len(xs):
        swap = (index & bit) != 0
        xs = [jnp.where(swap, xs[i ^ bit], xs[i]) for i in range(len(xs))]
        bit *= 2
    return xs


def pick(flag, a, b):
    flag, a, b = lax.optimization_barrier((flag, a, b))
    return jnp.where(flag, a, b)


def dot(a, b, dims):
    return lax.dot_general(a, b, (dims, ((), ())), preferred_element_type=jnp.float32)


def make_local(n_seq, n_fsdp):
    half = n_seq // 2
    n_mid = n_fsdp // 4
    per_block = n_mid // half

    def send(x, target):
        pairs = []
        for z in range(n_seq):
            for f in range(n_fsdp):
                to = target(z, f)
                if to is not None:
                    pairs.append((z * n_fsdp + f, to[0] * n_fsdp + to[1]))
        return lax.ppermute(x, AXES, pairs)

    top = n_fsdp // 2

    def moves(z, f):
        return (f // top) != (z // half)

    def core(x):
        return send(x, lambda z, f: (z, f ^ 1))

    def plane(x, mask):
        return send(x, lambda z, f: (z, f ^ mask))

    def far(x):
        return send(x, lambda z, f: (z ^ half, f))

    def near(x, mask):
        return send(x, lambda z, f: (z ^ mask, f))

    def local(tokens, in_mask, out_mask, w_mean, w_sigma, grad_out):
        highest = lax.Precision.HIGH
        bf16, f32 = jnp.bfloat16, jnp.float32
        rows, width = tokens.shape
        head_count = w_mean.shape[1]
        columns = head_count * w_mean.shape[2]
        head_width = w_mean.shape[2] // 3
        z = lax.axis_index("seq")
        f = lax.axis_index("fsdp")
        z_high, z_low = z // half, z % half
        is_core, mid = f % 2, (f // 2) % n_mid
        stays = (f // top) == z_high

        near_mean = [near(w_mean, m) for m in range(1, half)]

        in_sign = (2 * in_mask - 1).astype(bf16)
        token_far = send(tokens, lambda z, f: (z ^ half, f ^ top) if moves(z, f) else None)
        chunk = rows // SIGN_CHUNKS
        sign_chunks = lax.optimization_barrier([in_sign[c * chunk : (c + 1) * chunk] for c in range(SIGN_CHUNKS)])
        sides = [send(x, lambda z, f: (z, f ^ top) if moves(z, f) else None) for x in sign_chunks]
        sign_far = [send(x, lambda z, f: None if moves(z, f) else (z ^ half, f)) for x in sides]

        near_sigma = [near(w_sigma, m) for m in range(1, half)]
        out_own = lax.optimization_barrier((2 * out_mask - 1).astype(bf16).reshape(rows, columns))
        out_arrived = far(out_own)
        out_near = [near(out_own, m) for m in range(1, half)]

        def gather(x):
            cut = x.shape[0] // 2
            across = plane(x, top)
            along = [plane(x, 2 * j) for j in range(1, n_mid)]
            pieces = [(x, across)]
            for j, piece in enumerate(along, 1):
                upper = plane(piece[:cut], top)
                lower = plane(across[cut:], 2 * j)
                pieces.append((piece, jnp.concatenate([upper, lower], axis=0)))
            own, other = [], []
            for a, b in pieces:
                flag, a, b = lax.optimization_barrier((stays, a, b))
                own.append(jnp.where(flag, a, b))
                other.append(jnp.where(flag, b, a))
            return own, other

        token_piece = pick(stays, tokens, token_far)
        tokens_own, tokens_far = gather(token_piece)
        signs = []
        for c in range(SIGN_CHUNKS):
            piece = pick(stays, sign_chunks[c], sign_far[c])
            signs.append(gather(piece))
        signs_own, signs_far = (
            [jnp.concatenate([signs[c][k][j] for c in range(SIGN_CHUNKS)]) for j in range(n_mid)] for k in range(2)
        )
        own_parts, far_parts = list(zip(tokens_own, signs_own)), list(zip(tokens_far, signs_far))
        cut = rows // 2

        order = mid ^ (z_low * per_block)

        def panel_of(blocks):
            pair = jnp.stack(blocks).reshape(n_mid, 2, width, columns)
            mine = lax.dynamic_index_in_dim(pair, is_core, 1, keepdims=False)
            theirs = lax.dynamic_index_in_dim(pair, 1 - is_core, 1, keepdims=False)
            theirs = core(theirs)
            return xor_list([jnp.concatenate([mine[i], theirs[i]], axis=-1) for i in range(n_mid)], order)

        panel = list(zip(panel_of([w_mean, *near_mean]), panel_of([w_sigma, *near_sigma])))

        high = f // top
        share = rows // n_mid
        ordered = [(xor_list(own, order), xor_list(other, order)) for own, other in ((tokens_own, tokens_far), (signs_own, signs_far))]

        def bring(m, own, other):
            parts = []
            for q in range(per_block):
                i = m * per_block + q
                whole = pick(high == 0, own[i], other[i])
                parts.append(lax.dynamic_slice_in_dim(whole, mid * share, share))
            parts = jnp.stack(parts)
            return near(parts, m)

        brought = [(bring(m, *ordered[0]), bring(m, *ordered[1])) for m in range(1, half)]

        out_sign = [lax.optimization_barrier(jnp.concatenate([out_own, core(out_own)], axis=-1))]
        out_late = lax.optimization_barrier((out_arrived, signs[-1][0][0]))[0]
        out_sign.append(jnp.concatenate([out_late, core(out_late)], axis=-1))
        out_near = [(x, near(out_arrived, m)) for m, x in enumerate(out_near, 1)]
        out_near = [jnp.stack(lax.optimization_barrier(x)) for x in out_near]
        near_sign = [jnp.concatenate([x, core(x)], axis=-1) for x in out_near]

        chunk = rows // CHUNKS

        def project(parts, k, c):
            part = slice(c * chunk, (c + 1) * chunk)
            mean = sum(dot(x[0][part], w[0], ((1,), (0,))) for x, w in zip(parts, panel))
            flipped = [x[0][part] * x[1][part] for x in parts]
            sigma = sum(dot(x, w[1], ((1,), (0,))) for x, w in zip(flipped, panel))
            both = mean + out_sign[k][part].astype(f32) * sigma
            return both[:, :columns] + core(both[:, columns:].astype(bf16)).astype(f32)

        from_far = []
        for c in range(CHUNKS):
            part = project(far_parts, 1, c)
            from_far.append(far(part.astype(bf16)))
        projected = jnp.concatenate([project(own_parts, 0, c) + from_far[c].astype(f32) for c in range(CHUNKS)])
        projected = projected.reshape(rows, head_count, 3 * head_width).transpose(1, 0, 2)

        near_pieces = []
        for x in brought:
            x = jnp.stack(lax.optimization_barrier(x))
            across = plane(x, top)
            along = [plane(x, 2 * j) for j in range(1, n_mid)]
            ends = [y[:, :, : share // 2] for y in along]
            start = across[:, :, share // 2 :]
            upper = [plane(y, top) for y in ends]
            lower = [plane(start, 2 * j) for j in range(1, n_mid)]
            near_pieces.append((x, across, along, upper, lower))

        pre_query = projected[:, :, :head_width]
        pre_keys = projected[:, :, head_width : 2 * head_width]
        queries = feature_map(pre_query)
        key_feats = feature_map(pre_keys)
        values = projected[:, :, 2 * head_width :]
        causal = (
            lax.broadcasted_iota(jnp.int32, (rows, rows), 0)
            >= lax.broadcasted_iota(jnp.int32, (rows, rows), 1)
        ).astype(f32)
        state = jnp.einsum("hse,hsf->hef", key_feats, values, precision=highest).astype(bf16)
        incoming = sum(
            jnp.where(z >= k, send(state, lambda z, f, k=k: ((z + k) % n_seq, f)).astype(f32), 0.0)
            for k in range(1, n_seq)
        )
        scores = jnp.einsum("hte,hse->hts", queries, key_feats, precision=highest) * causal
        numerator = jnp.einsum("hts,hsf->htf", scores, values, precision=highest)
        numerator = numerator + jnp.einsum("hte,hef->htf", queries, incoming, precision=highest)
        inv_norm = lax.rsqrt(jnp.mean(numerator * numerator, axis=-1, keepdims=True) + EPSILON)
        normed = numerator * inv_norm
        attended = normed.transpose(1, 0, 2).reshape(rows, head_count * head_width).astype(bf16)
        upstream = grad_out.astype(f32).reshape(rows, head_count, head_width).transpose(1, 0, 2)
        d_numer = inv_norm * (upstream - normed * jnp.mean(upstream * normed, axis=-1, keepdims=True))
        back_state = jnp.einsum("hte,htf->hef", queries, d_numer, precision=highest).astype(bf16)
        suffix = sum(
            jnp.where(z + k < n_seq, send(back_state, lambda z, f, k=k: ((z - k) % n_seq, f)).astype(f32), 0.0)
            for k in range(1, n_seq)
        )
        d_scores = jnp.einsum("htf,hsf->hts", d_numer, values, precision=highest) * causal
        d_query = jnp.einsum("hts,hse->hte", d_scores, key_feats, precision=highest)
        d_query = d_query + jnp.einsum("hef,htf->hte", incoming, d_numer, precision=highest)
        d_keys = jnp.einsum("hts,hte->hse", d_scores, queries, precision=highest)
        d_keys = d_keys + jnp.einsum("hef,hsf->hse", suffix, values, precision=highest)
        d_values = jnp.einsum("hts,htf->hsf", scores, d_numer, precision=highest)
        d_values = d_values + jnp.einsum("hef,hse->hsf", suffix, key_feats, precision=highest)
        grad_pre = jnp.concatenate(
            [d_query * feature_slope(pre_query), d_keys * feature_slope(pre_keys), d_values], axis=-1
        )
        grad_own = grad_pre.transpose(1, 0, 2).reshape(rows, columns).astype(bf16)

        near_own = [near(grad_own, m) for m in range(1, half)]
        grad_far = far(grad_own)
        near_far = [near(grad_far, m) for m in range(1, half)]

        def widened(grad, sign):
            wide, sign = lax.optimization_barrier((jnp.concatenate([grad, core(grad)], axis=-1), sign))
            return wide, wide * sign

        own_wide, far_wide = widened(grad_own, out_sign[0]), widened(grad_far, out_sign[1])
        wides, flips = zip(own_wide, far_wide)

        def row_sum(parts, k):
            sums = None
            for j in range(n_mid):
                back = dot(wides[k], panel[j][0], ((1,), (1,)))
                back = back + parts[j][1].astype(f32) * dot(flips[k], panel[j][1], ((1,), (1,)))
                if j:
                    back = plane(back.astype(bf16), 2 * j).astype(f32)
                sums = back if sums is None else sums + back
            return sums

        own_sum = row_sum(own_parts, 0)
        own_y = send(own_sum.astype(bf16), lambda z, f: (z, f ^ top) if moves(z, f) else None)
        own_sum = own_sum + own_y.astype(f32)

        far_half = None
        for j in reversed(range(n_mid)):
            back = dot(far_wide[0], panel[j][0], ((1,), (1,)))
            back = back + far_parts[j][1].astype(f32) * dot(far_wide[1], panel[j][1], ((1,), (1,)))
            mine = jnp.where(stays, back[:cut], back[cut:])
            other = jnp.where(stays, back[cut:], back[:cut]).astype(bf16)
            arrived = plane(other, top + 2 * j).astype(f32)
            if j:
                arrived = arrived + plane(mine.astype(bf16), 2 * j).astype(f32)
            else:
                arrived = arrived + mine
            far_half = arrived if far_half is None else far_half + arrived
        far_half = far_half.astype(bf16)
        last_back = other
        first = send(far_half, lambda z, f: None if moves(z, f) else (z ^ half, f))
        second = send(far_half, lambda z, f: (z ^ half, f ^ top) if moves(z, f) else None)
        own_sum = lax.optimization_barrier(own_sum.astype(bf16))
        d_tokens = jnp.concatenate([jnp.where(stays, own_sum[:cut], first), jnp.where(stays, own_sum[cut:], second)])
        near_rows = []
        for pieces in near_pieces:
            x, across, along, upper, lower = lax.optimization_barrier((pieces, last_back))[0]
            mine = jnp.concatenate(xor_list([x, *along], mid), axis=2)
            ends = [jnp.concatenate(pair, axis=2) for pair in zip(upper, lower)]
            other = jnp.concatenate(xor_list([across, *ends], mid), axis=2)
            near_rows.append((jnp.where(high == 0, mine, other), jnp.where(high == 0, other, mine)))
        terms = [(own_wide, [(ordered[0][0][q], ordered[1][0][q]) for q in range(per_block)])]
        terms.append((far_wide, [(ordered[0][1][q], ordered[1][1][q]) for q in range(per_block)]))
        for grads, k in ((near_own, 0), (near_far, 1)):
            for grad, sign, pieces in zip(grads, near_sign, near_rows):
                pair = [(pieces[k][0, q], pieces[k][1, q]) for q in range(per_block)]
                terms.append((widened(grad, sign[k]), pair))
        sums = None
        for g, x in terms:
            part = [dot(x[q][0], g[0], ((0,), (0,))) for q in range(per_block)]
            part += [dot(x[q][0] * x[q][1], g[1], ((0,), (0,))) for q in range(per_block)]
            sums = part if sums is None else [a + b for a, b in zip(sums, part)]
        total = jnp.stack(sums).reshape(2, per_block, width, 2 * columns).astype(bf16)
        kept, given = total[..., :columns], core(total[..., columns:])
        full = jnp.stack([jnp.where(is_core == 0, kept, given), jnp.where(is_core == 0, given, kept)], axis=2)
        g_mean, g_sigma = (full[k].reshape(w_mean.shape) for k in range(2))
        return attended, d_tokens, g_mean, g_sigma

    return local


def solution(mesh):
    placed = (
        P("seq", "fsdp"),
        P("seq", "fsdp"),
        P("seq", "fsdp", None),
        P("seq", "fsdp", None),
        P("seq", "fsdp", None),
        P("seq", "fsdp"),
    )
    return jax.shard_map(
        make_local(mesh.shape["seq"], mesh.shape["fsdp"]),
        mesh=mesh,
        in_specs=placed,
        out_specs=(
            P("seq", "fsdp"),
            P("seq", "fsdp"),
            P("seq", "fsdp", None),
            P("seq", "fsdp", None),
        ),
        check_vma=False,
    )
```
